32 devices in a mesh: grp: 4 (over y, core), shard: 8 (over z, x).
Axes of the slice: x: 2, y: 2, z: 4, core: 2. Of those that a mesh axis runs over, the one named last changes fastest.
Arguments:
- events: bfloat16 [4096, 1024], P(('grp', 'shard')), may hold values from -6 to 6
- user_ids: int32 [4096], P(('grp', 'shard')), may hold values from 0 to 31, as said below
- session_break: int32 [4096], P(('grp', 'shard')), may hold values 0 or 1
- in_gain: float32 [1024], replicated, may hold values from 0.1 to 1.9
- in_weight: bfloat16 [1024, 2048], replicated, may hold values from -0.1875 to 0.1875
- decay_rates: float32 [1024], replicated, may hold values from 0.0001 to 0.04
- keep_factor: float32 [1024], replicated, may hold values from 0.4 to 0.8
- out_gain: float32 [1024], replicated, may hold values from 0.1 to 1.9
- out_weight: bfloat16 [1024, 1024], replicated, may hold values from -0.1875 to 0.1875
Outputs:
- mixed: bfloat16 [4096, 1024], P(('grp', 'shard'))
The draws below stay inside these ranges and needn't reach their ends.
Inputs may be any that keep to these rules, and one draw needn't show every extreme that they name: The owner range of an event is user_ids // 4. In every aligned block of 128 rows at most 34 rows share an owner range; in every aligned stretch of 1024 rows one owner range has exactly 34 rows in each of its blocks.
All inputs are finite; a program needn't handle non-finite values. No bound on the sum of `session_break` on one device may be relied on, other than what follows from the above.
Results may differ from the reference program's by a relative error of at most 0.0057.
Values may be sent and summed in bfloat16 or wider, within the bound.
No kernel may reach another device: no remote copies, remote signals or barrier semaphores. Data moves between devices by JAX's collectives and lax.ppermute only.
A program may use at most 64 MiB of HBM per device.

```python
import jax
import jax.numpy as jnp
from jax import lax

D = 1024
EV_DEV = 128
U_DEV = 4
WINDOW = 1024
EVENTS = 4096
USERS = 32
CAP = 34


def draw_user_ids(key, part):
    owners = USERS // U_DEV
    groups = EVENTS // WINDOW
    blocks = EVENTS // EV_DEV
    full_owner = jax.random.randint(jax.random.fold_in(key, 1), (groups,), 0, owners)
    full_block = jnp.repeat(full_owner, owners)

    def one_block(block_key, full_dest):
        pool_index = jax.random.permutation(jax.random.fold_in(block_key, 0), (owners - 1) * CAP)[:EV_DEV - CAP]
        other_owner = (full_dest + 1 + pool_index // CAP) % owners
        owner_list = jnp.concatenate([jnp.full((CAP,), full_dest, jnp.int32), other_owner.astype(jnp.int32)])
        shuffle_order = jax.random.permutation(jax.random.fold_in(block_key, 1), EV_DEV)
        owner_list = owner_list[shuffle_order]
        local_user = jax.random.randint(jax.random.fold_in(block_key, 2), (EV_DEV,), 0, U_DEV)
        return (owner_list * U_DEV + local_user).astype(jnp.int32)
    block_keys = jax.random.split(jax.random.fold_in(key, 2), blocks)
    return jax.vmap(one_block)(block_keys, full_block).reshape(EVENTS)


def draw_decay_rates(key, part):
    key_one = jax.random.fold_in(key, 11)
    return jnp.exp(jax.random.uniform(key_one, (D,), jnp.float32, jnp.log(0.001), jnp.log(0.04)))


def place_ends(entries, stream_key, smallest, largest):
    longest = entries.shape.index(max(entries.shape))
    spots = []
    for shift in (0, 1):
        where = [jax.random.randint(jax.random.fold_in(stream_key, axis), (), 0, length) for axis, length in enumerate(entries.shape)]
        where[longest] = (where[longest] + shift) % entries.shape[longest]
        spots.append(tuple(where))
    return entries.at[spots[0]].set(smallest).at[spots[1]].set(largest)


def block_scale(stream_key, shape, shards, smallest, high):
    level = 1.0
    for dim, shards_of in shards:
        heights = jax.random.uniform(jax.random.fold_in(jax.random.fold_in(stream_key, 6), dim), (shards_of,), jnp.float32, smallest / len(shards), high / len(shards))
        level = level * jnp.repeat(jnp.exp(heights), shape[dim] // shards_of).reshape((-1,) + (1,) * (len(shape) - 1 - dim))
    return level


def normal_values(stream_key, dims, spread, reach, shards=(), kind=jnp.bfloat16):
    array = jax.random.normal(stream_key, dims, jnp.float32) * spread
    if len(shards) > 0:
        array = block_scale(stream_key, dims, shards, -0.22, 0.18) * array
    return jnp.clip(array, min=-reach, max=reach).astype(kind)


def setup_inputs(seed: int = 0) -> dict:
    key_list = jax.random.split(jax.random.key(seed), 10)
    return {
        "events": normal_values(key_list[0], (EVENTS, D), 1.0, 6.0, ((0, 32),)),
        "user_ids": draw_user_ids(jax.random.fold_in(key_list[9], 71), 0),
        "session_break": place_ends((jax.random.randint(key_list[2], (EVENTS,), 0, 96) < 1).astype(jnp.int32), jax.random.fold_in(key_list[2], 1), 0, 1),
        "in_gain": jnp.clip(1.0 + 0.18 * jax.random.normal(key_list[3], (D,), jnp.float32), 0.1, 1.9),
        "in_weight": normal_values(key_list[4], (D, 2 * D), D ** -0.5, 0.1875),
        "decay_rates": draw_decay_rates(jax.random.fold_in(key_list[9], 71), 0),
        "keep_factor": jnp.clip(jax.random.uniform(key_list[6], (D,), jnp.float32, 0.4, 0.8), 0.4, 0.8),
        "out_gain": jnp.clip(1.0 + 0.18 * jax.random.normal(key_list[7], (D,), jnp.float32), 0.1, 1.9),
        "out_weight": normal_values(key_list[8], (D, D), D ** -0.5, 0.1875),
    }


def rms_scale(values, gain_vec):
    return values * lax.rsqrt(lax.optimization_barrier(jnp.mean(values * values, axis=-1, keepdims=True)) + 1e-06) * gain_vec

def reference(events, user_ids, session_break, in_gain, in_weight, decay_rates, keep_factor, out_gain, out_weight):
    event_rows = events.astype(jnp.float32)
    normed = rms_scale(event_rows, in_gain).astype(jnp.bfloat16)
    projected = jnp.dot(normed, in_weight, preferred_element_type=jnp.float32).astype(jnp.bfloat16)
    gate_part = projected[:, :D].astype(jnp.float32)
    base_decay = jnp.exp(-decay_rates)

    def advance(carry_state, step_item):
        user_now, break_now, value_now = step_item
        factor = base_decay * jnp.where(break_now == 1, keep_factor, jnp.ones_like(keep_factor))
        state_new = factor * carry_state[user_now] + value_now.astype(jnp.float32)
        return (carry_state.at[user_now].set(state_new), state_new)
    state_zero = jnp.zeros((USERS, D), decay_rates.dtype)
    _, hidden = lax.scan(advance, state_zero, (user_ids, session_break, projected[:, D:]))
    mixed_part = (rms_scale(hidden, out_gain) * jax.nn.silu(gate_part)).astype(jnp.bfloat16)
    return (event_rows + jnp.dot(mixed_part, out_weight, preferred_element_type=jnp.float32)).astype(jnp.bfloat16)
```

```python
import functools

import jax
import jax.numpy as jnp
from jax import lax
from jax.experimental import pallas as pl
from jax.experimental.pallas import tpu as pltpu
from jax.sharding import PartitionSpec as P

U_DEV = 4
LANES = 128
AXES = ("grp", "shard")
F32, BF16 = jnp.float32, jnp.bfloat16


def round_up(value, unit):
    return -(-value // unit) * unit


def dot(left, right):
    return jnp.dot(left, right, preferred_element_type=F32)


def dot_t(left, right):
    return lax.dot_general(left, right, (((0,), (0,)), ((), ())), preferred_element_type=F32)


def rms_rows(values):
    return lax.rsqrt(jnp.mean(values * values, axis=-1, keepdims=True) + 1e-06)


def member_rows(ids_row, users):
    user = lax.broadcasted_iota(jnp.int32, (users, ids_row.shape[1]), 0)
    return (user == ids_row).astype(F32)


def weight_copies(hbm, vmem, sem, chunks, first):
    width = vmem.shape[1] // chunks
    return [
        pltpu.make_async_copy(
            hbm.at[:, pl.ds(first + c * width, width)],
            vmem.at[:, pl.ds(c * width, width)],
            sem.at[c],
        )
        for c in range(chunks)
    ]


def ends_kernel(
    users, rows_used, chunks,
    events, ids, breaks, in_gain, rates, keep, weight,
    payload, normed_out, value_out,
    held, stage, sem,
):
    rows, width = events.shape
    copies = weight_copies(weight, held, sem, chunks, width)
    for copy in copies:
        copy.start()
    ids_row = ids[...]
    break_row = breaks[...].astype(F32)
    member = member_rows(ids_row, users)
    member_b = member.astype(BF16)
    same = dot_t(member_b, member_b)
    after = lax.broadcasted_iota(jnp.int32, (rows, rows), 1) > lax.broadcasted_iota(
        jnp.int32, (rows, rows), 0
    )
    later = jnp.where(after, same, 0.0)
    events_left = jnp.sum(later, axis=1, keepdims=True)
    breaks_left = jnp.sum(later * break_row, axis=1, keepdims=True)
    user_events = jnp.sum(member, axis=1, keepdims=True)
    user_breaks = jnp.sum(member * break_row, axis=1, keepdims=True)
    event_rows = events[...].astype(F32)
    normed = (event_rows * rms_rows(event_rows) * in_gain[...]).astype(BF16)
    normed_out[...] = normed
    splits = width // (rows_used * LANES)
    for s in range(splits):
        stage[:, s, rows_used, :] = jnp.broadcast_to(user_events, (users, LANES))
        stage[:, s, rows_used + 1, :] = jnp.broadcast_to(user_breaks, (users, LANES))
        for r in range(rows_used + 2, stage.shape[2]):
            stage[:, s, r, :] = jnp.zeros((users, LANES), F32)
    block = width // chunks
    for c in range(chunks):
        copies[c].wait()
        cols = pl.ds(c * block, block)
        value = dot(normed, held[:, cols]).astype(BF16)
        value_out[:, cols] = value
        log_left = -rates[:, cols] * events_left + jnp.log(keep[:, cols]) * breaks_left
        faded = (jnp.exp(log_left) * value.astype(F32)).astype(BF16)
        ends = dot(member_b, faded)
        for k in range(block // LANES):
            tile = c * (block // LANES) + k
            stage[:, tile // rows_used, tile % rows_used, :] = ends[:, k * LANES:(k + 1) * LANES]
    payload[...] = stage[...].astype(BF16)


def local_kernel(
    users, chunks,
    normed, value, ids, breaks, rates, keep, out_gain, weight,
    gate_out, growth_out, local_out,
    held, sem,
):
    rows, width = normed.shape
    copies = weight_copies(weight, held, sem, chunks, 0)
    for copy in copies:
        copy.start()
    break_row = breaks[...].astype(F32)
    member_b = member_rows(ids[...], users).astype(BF16)
    same = dot_t(member_b, member_b)
    upto = lax.broadcasted_iota(jnp.int32, (rows, rows), 1) <= lax.broadcasted_iota(
        jnp.int32, (rows, rows), 0
    )
    within = jnp.where(upto, same, 0.0)
    count = jnp.sum(within, axis=1, keepdims=True)
    count_breaks = jnp.sum(within * break_row, axis=1, keepdims=True)
    within_b = within.astype(BF16)
    within_twice = jnp.concatenate([within_b, within_b], axis=1)
    block = width // chunks
    for c in range(chunks):
        cols = pl.ds(c * block, block)
        log_level = -rates[:, cols] * count + jnp.log(keep[:, cols]) * count_breaks
        growth = jnp.exp(log_level)
        growth_out[:, cols] = growth
        scaled = jnp.exp(-log_level) * value[:, cols].astype(F32)
        high = scaled.astype(BF16)
        low = (scaled - high.astype(F32)).astype(BF16)
        local_out[:, cols] = growth * dot(within_twice, jnp.concatenate([high, low], axis=0))
    for c in range(chunks):
        copies[c].wait()
        cols = pl.ds(c * block, block)
        gate = dot(normed[...], held[:, cols]).astype(BF16).astype(F32)
        gate_out[:, cols] = out_gain[:, cols] * (gate / (1.0 + jnp.exp(-gate)))


def prefix_kernel(rows_used, got, rates, keep, carries):
    devices = got.shape[0]
    rate = rates[...]
    log_keep = jnp.log(keep[...])
    pad = carries.shape[1] - rows_used

    def step(d, state):
        block = got[d].astype(F32)
        stored = state
        if pad:
            stored = jnp.concatenate([state, jnp.zeros((pad, LANES), F32)], axis=0)
        carries[d] = stored.astype(BF16)
        span = jnp.exp(
            -rate * block[rows_used:rows_used + 1] + log_keep * block[rows_used + 1:rows_used + 2]
        )
        return span * state + block[:rows_used]

    state = jnp.zeros((rows_used, LANES), F32)
    if devices <= 64:
        for d in range(devices):
            state = step(d, state)
    else:
        lax.fori_loop(0, devices, step, state)


def final_kernel(
    users, rows_used, chunks,
    carries, ids, local, growth, gate, events, weight,
    out,
    held, stage, sem,
):
    rows, width = events.shape
    copies = weight_copies(weight, held, sem, chunks, 0)
    for copy in copies:
        copy.start()
    member_b = member_rows(ids[...], users).astype(BF16)
    stage[...] = carries[...].astype(F32)
    tiles = [
        stage[:, t // rows_used, t % rows_used, :].astype(BF16) for t in range(width // LANES)
    ]
    carry = dot_t(member_b, jnp.concatenate(tiles, axis=1))
    state = local[...] + growth[...] * carry
    mixed_part = (state * rms_rows(state) * gate[...]).astype(BF16)
    block = width // chunks
    for c in range(chunks):
        copies[c].wait()
        cols = pl.ds(c * block, block)
        out[:, cols] = (events[:, cols].astype(F32) + dot(mixed_part, held[:, cols])).astype(BF16)


def on_device(
    devices,
    owners,
    events,
    user_ids,
    session_break,
    in_gain,
    in_weight,
    decay_rates,
    keep_factor,
    out_gain,
    out_weight,
):
    rows, width = events.shape
    users = U_DEV * owners
    rows_used = users * width // (devices * LANES)
    splits = width // (rows_used * LANES)
    rows_out = round_up(rows_used + 2, 8)
    rows_back = round_up(rows_used, 8)
    chunks = 4
    ids = user_ids.reshape(1, rows)
    breaks = session_break.reshape(1, rows)
    row = lambda vector: vector.reshape(1, width)
    hbm = pl.BlockSpec(memory_space=pl.ANY)
    vmem = pl.BlockSpec(memory_space=pltpu.VMEM)
    sds = jax.ShapeDtypeStruct

    payload, normed, value = pl.pallas_call(
        functools.partial(ends_kernel, users, rows_used, chunks),
        out_shape=(
            sds((users, splits, rows_out, LANES), BF16),
            sds((rows, width), BF16),
            sds((rows, width), BF16),
        ),
        in_specs=[vmem] * 6 + [hbm],
        out_specs=(vmem, vmem, vmem),
        scratch_shapes=[
            pltpu.VMEM((width, width), BF16),
            pltpu.VMEM((users, splits, rows_out, LANES), F32),
            pltpu.SemaphoreType.DMA((chunks,)),
        ],
        cost_estimate=pl.CostEstimate(
            flops=2 * rows * width * width, bytes_accessed=2 * width * width, transcendentals=0
        ),
        name="ends",
    )(events, ids, breaks, row(in_gain), row(decay_rates), row(keep_factor), in_weight)
    got = lax.all_to_all(
        payload.reshape(devices, rows_out, LANES), AXES, split_axis=0, concat_axis=0, tiled=True
    )
    gate, growth, local = pl.pallas_call(
        functools.partial(local_kernel, users, chunks),
        out_shape=(sds((rows, width), F32),) * 3,
        in_specs=[vmem] * 7 + [hbm],
        out_specs=(vmem, vmem, vmem),
        scratch_shapes=[
            pltpu.VMEM((width, width), BF16),
            pltpu.SemaphoreType.DMA((chunks,)),
        ],
        cost_estimate=pl.CostEstimate(
            flops=2 * rows * width * width, bytes_accessed=2 * width * width, transcendentals=0
        ),
        name="local",
    )(normed, value, ids, breaks, row(decay_rates), row(keep_factor), row(out_gain), in_weight)
    if splits == 1:
        own = lambda vector: vector.reshape(rows_used, LANES)
    else:
        part = lax.axis_index(AXES) % splits
        own = lambda vector: lax.dynamic_index_in_dim(
            vector.reshape(splits, rows_used, LANES), part, 0, keepdims=False
        )
    carries = pl.pallas_call(
        functools.partial(prefix_kernel, rows_used),
        out_shape=sds((devices, rows_back, LANES), BF16),
        in_specs=[vmem] * 3,
        out_specs=vmem,
        name="prefix",
    )(got, own(decay_rates), own(keep_factor))
    back = lax.all_to_all(carries, AXES, split_axis=0, concat_axis=0, tiled=True)
    return pl.pallas_call(
        functools.partial(final_kernel, users, rows_used, chunks),
        out_shape=sds((rows, width), BF16),
        in_specs=[vmem] * 6 + [hbm],
        out_specs=vmem,
        scratch_shapes=[
            pltpu.VMEM((width, width), BF16),
            pltpu.VMEM((users, splits, rows_back, LANES), F32),
            pltpu.SemaphoreType.DMA((chunks,)),
        ],
        cost_estimate=pl.CostEstimate(
            flops=2 * rows * width * width, bytes_accessed=2 * width * width, transcendentals=0
        ),
        name="final",
    )(back.reshape(users, splits, rows_back, LANES), ids, local, growth, gate, events, out_weight)


def solution(mesh):
    return jax.shard_map(
        functools.partial(on_device, mesh.size, mesh.shape["shard"]),
        mesh=mesh,
        in_specs=(P(AXES, None), P(AXES), P(AXES), P(), P(), P(), P(), P(), P()),
        out_specs=P(AXES, None),
        check_vma=False,
    )
```

```python
import functools

import jax
import jax.numpy as jnp
from jax import lax
from jax.experimental import pallas as pl
from jax.experimental.pallas import tpu as pltpu
from jax.sharding import PartitionSpec as P

U_DEV = 4
LANES = 128
CHUNKS = 4
VMEM_BYTES = 12 * 2**20
AXES = ("grp", "shard")
F32, BF16 = jnp.float32, jnp.bfloat16


def round_up(value, unit):
    return -(-value // unit) * unit


def dot(left, right):
    return jnp.dot(left, right, preferred_element_type=F32)


def dot_t(left, right):
    return lax.dot_general(left, right, (((0,), (0,)), ((), ())), preferred_element_type=F32)


def rms_rows(values):
    return lax.rsqrt(jnp.mean(values * values, axis=-1, keepdims=True) + 1e-06)


def normed_rows(events, in_gain):
    event_rows = events[...].astype(F32)
    return (event_rows * rms_rows(event_rows) * in_gain[...]).astype(BF16)


def member_rows(ids_row, users):
    user = lax.broadcasted_iota(jnp.int32, (users, ids_row.shape[1]), 0)
    return (user == ids_row).astype(F32)


def started(copies):
    for copy in copies:
        copy.start()
    return copies


def weight_copies(hbm, vmem, sem, chunks, first):
    width = vmem.shape[1] // chunks
    return [
        pltpu.make_async_copy(
            hbm.at[:, pl.ds(first + c * width, width)],
            vmem.at[:, pl.ds(c * width, width)],
            sem.at[c],
        )
        for c in range(chunks)
    ]


def ends_kernel(
    users, rows_used,
    events_hbm, ids_hbm, breaks_hbm, in_gain_hbm, rates_hbm, keep_hbm, weight_hbm,
    payload,
    events, ids, breaks, in_gain, rates, keep, held, stage, small_sem, sem,
):
    rows, width = events.shape
    small = started(
        [
            pltpu.make_async_copy(source, target, small_sem.at[i])
            for i, (source, target) in enumerate(
                (
                    (events_hbm, events),
                    (ids_hbm, ids),
                    (breaks_hbm, breaks),
                    (in_gain_hbm, in_gain),
                    (rates_hbm, rates),
                    (keep_hbm, keep),
                )
            )
        ]
    )
    copies = started(weight_copies(weight_hbm, held, sem, CHUNKS, width))
    for copy in small:
        copy.wait()
    break_row = breaks[...].astype(F32)
    member = member_rows(ids[...], users)
    member_b = member.astype(BF16)
    same = dot_t(member_b, member_b)
    after = lax.broadcasted_iota(jnp.int32, (rows, rows), 1) > lax.broadcasted_iota(
        jnp.int32, (rows, rows), 0
    )
    later = jnp.where(after, same, 0.0)
    events_left = jnp.sum(later, axis=1, keepdims=True)
    breaks_left = jnp.sum(later * break_row, axis=1, keepdims=True)
    user_events = jnp.sum(member, axis=1, keepdims=True)
    user_breaks = jnp.sum(member * break_row, axis=1, keepdims=True)
    normed = normed_rows(events, in_gain)
    splits = width // (rows_used * LANES)
    for s in range(splits):
        stage[:, s, rows_used, :] = jnp.broadcast_to(user_events, (users, LANES))
        stage[:, s, rows_used + 1, :] = jnp.broadcast_to(user_breaks, (users, LANES))
        for r in range(rows_used + 2, stage.shape[2]):
            stage[:, s, r, :] = jnp.zeros((users, LANES), F32)
    block = width // CHUNKS
    for c in range(CHUNKS):
        cols = pl.ds(c * block, block)
        fade = jnp.exp(-rates[:, cols] * events_left + jnp.log(keep[:, cols]) * breaks_left)
        copies[c].wait()
        value = dot(normed, held[:, cols]).astype(BF16)
        ends = dot(member_b, (fade * value.astype(F32)).astype(BF16))
        for k in range(block // LANES):
            tile = c * (block // LANES) + k
            stage[:, tile // rows_used, tile % rows_used, :] = ends[:, k * LANES:(k + 1) * LANES]
    payload[...] = stage[...].astype(BF16)


def local_kernel(
    users,
    events, ids, breaks, in_gain, rates, keep, out_gain, weight_hbm,
    held_back,
    held, sem,
):
    rows, width = events.shape
    copies = started(weight_copies(weight_hbm, held, sem, 2 * CHUNKS, 0))
    break_row = breaks[...].astype(F32)
    member_b = member_rows(ids[...], users).astype(BF16)
    same = dot_t(member_b, member_b)
    upto = lax.broadcasted_iota(jnp.int32, (rows, rows), 1) <= lax.broadcasted_iota(
        jnp.int32, (rows, rows), 0
    )
    within = jnp.where(upto, same, 0.0)
    count = jnp.sum(within, axis=1, keepdims=True)
    count_breaks = jnp.sum(within * break_row, axis=1, keepdims=True)
    within_b = within.astype(BF16)
    within_twice = jnp.concatenate([within_b, within_b], axis=1)
    normed = normed_rows(events, in_gain)
    block = width // CHUNKS
    for c in range(CHUNKS):
        copies[c].wait()
        cols = pl.ds(c * block, block)
        gate = dot(normed, held[:, cols]).astype(BF16).astype(F32)
        held_back[0, :, cols] = out_gain[:, cols] * (gate / (1.0 + jnp.exp(-gate)))
    for c in range(CHUNKS):
        cols = pl.ds(c * block, block)
        log_level = -rates[:, cols] * count + jnp.log(keep[:, cols]) * count_breaks
        growth = jnp.exp(log_level)
        held_back[1, :, cols] = growth
        copies[CHUNKS + c].wait()
        value = dot(normed, held[:, pl.ds(width + c * block, block)]).astype(BF16)
        scaled = jnp.exp(-log_level) * value.astype(F32)
        high = scaled.astype(BF16)
        low = (scaled - high.astype(F32)).astype(BF16)
        held_back[2, :, cols] = growth * dot(within_twice, jnp.concatenate([high, low], axis=0))


def prefix_kernel(rows_used, got, rates, keep, carries):
    devices = got.shape[0]
    rate = rates[...]
    log_keep = jnp.log(keep[...])
    pad = carries.shape[1] - rows_used

    def step(d, state):
        block = got[d].astype(F32)
        stored = state
        if pad:
            stored = jnp.concatenate([state, jnp.zeros((pad, LANES), F32)], axis=0)
        carries[d] = stored.astype(BF16)
        span = jnp.exp(
            -rate * block[rows_used:rows_used + 1] + log_keep * block[rows_used + 1:rows_used + 2]
        )
        return span * state + block[:rows_used]

    state = jnp.zeros((rows_used, LANES), F32)
    if devices <= 64:
        for d in range(devices):
            state = step(d, state)
    else:
        lax.fori_loop(0, devices, step, state)


def final_kernel(
    users, rows_used,
    carries, ids, held_back, events_hbm, weight_hbm,
    out,
    events, held, stage, small_sem, sem,
):
    rows, width = events.shape
    copies = started(weight_copies(weight_hbm, held, sem, CHUNKS, 0))
    (events_copy,) = started([pltpu.make_async_copy(events_hbm, events, small_sem)])
    member_b = member_rows(ids[...], users).astype(BF16)
    stage[...] = carries[...].astype(F32)
    tiles = [
        stage[:, t // rows_used, t % rows_used, :].astype(BF16) for t in range(width // LANES)
    ]
    carry = dot_t(member_b, jnp.concatenate(tiles, axis=1))
    state = held_back[2] + held_back[1] * carry
    mixed_part = (state * rms_rows(state) * held_back[0]).astype(BF16)
    block = width // CHUNKS
    events_copy.wait()
    for c in range(CHUNKS):
        copies[c].wait()
        cols = pl.ds(c * block, block)
        out[:, cols] = (events[:, cols].astype(F32) + dot(mixed_part, held[:, cols])).astype(BF16)


def on_device(
    devices,
    owners,
    events,
    user_ids,
    session_break,
    in_gain,
    in_weight,
    decay_rates,
    keep_factor,
    out_gain,
    out_weight,
):
    rows, width = events.shape
    users = U_DEV * owners
    rows_used = users * width // (devices * LANES)
    splits = width // (rows_used * LANES)
    rows_out = round_up(rows_used + 2, 8)
    rows_back = round_up(rows_used, 8)
    ids = user_ids.reshape(1, rows)
    breaks = session_break.reshape(1, rows)
    row = lambda vector: vector.reshape(1, width)
    hbm = pl.BlockSpec(memory_space=pltpu.HBM)
    vmem = pl.BlockSpec(memory_space=pltpu.VMEM)
    in_hbm = lambda value: pltpu.with_memory_space_constraint(value, pltpu.HBM)
    sds = jax.ShapeDtypeStruct
    params = pltpu.CompilerParams(vmem_limit_bytes=VMEM_BYTES)
    half = pl.CostEstimate(
        flops=2 * rows * width * width, bytes_accessed=2 * width * width, transcendentals=0
    )
    whole = pl.CostEstimate(
        flops=4 * rows * width * width, bytes_accessed=4 * width * width, transcendentals=0
    )

    payload = pl.pallas_call(
        functools.partial(ends_kernel, users, rows_used),
        out_shape=sds((users, splits, rows_out, LANES), BF16),
        in_specs=[hbm] * 7,
        out_specs=vmem,
        scratch_shapes=[
            pltpu.VMEM((rows, width), BF16),
            pltpu.VMEM((1, rows), jnp.int32),
            pltpu.VMEM((1, rows), jnp.int32),
            pltpu.VMEM((1, width), F32),
            pltpu.VMEM((1, width), F32),
            pltpu.VMEM((1, width), F32),
            pltpu.VMEM((width, width), BF16),
            pltpu.VMEM((users, splits, rows_out, LANES), F32),
            pltpu.SemaphoreType.DMA((6,)),
            pltpu.SemaphoreType.DMA((CHUNKS,)),
        ],
        cost_estimate=half,
        compiler_params=params,
        name="ends",
    )(*map(in_hbm, (events, ids, breaks, row(in_gain), row(decay_rates), row(keep_factor), in_weight)))
    got = lax.all_to_all(
        payload.reshape(devices, rows_out, LANES), AXES, split_axis=0, concat_axis=0, tiled=True
    )
    held_back = pl.pallas_call(
        functools.partial(local_kernel, users),
        out_shape=sds((3, rows, width), F32),
        in_specs=[vmem] * 7 + [hbm],
        out_specs=vmem,
        scratch_shapes=[
            pltpu.VMEM((width, 2 * width), BF16),
            pltpu.SemaphoreType.DMA((2 * CHUNKS,)),
        ],
        cost_estimate=whole,
        compiler_params=params,
        name="local",
    )(
        events, ids, breaks, row(in_gain), row(decay_rates), row(keep_factor), row(out_gain),
        in_hbm(in_weight),
    )
    if splits == 1:
        own = lambda vector: vector.reshape(rows_used, LANES)
    else:
        part = lax.axis_index(AXES) % splits
        own = lambda vector: lax.dynamic_index_in_dim(
            vector.reshape(splits, rows_used, LANES), part, 0, keepdims=False
        )
    carries = pl.pallas_call(
        functools.partial(prefix_kernel, rows_used),
        out_shape=sds((devices, rows_back, LANES), BF16),
        in_specs=[vmem] * 3,
        out_specs=vmem,
        compiler_params=params,
        name="prefix",
    )(got, own(decay_rates), own(keep_factor))
    back = lax.all_to_all(carries, AXES, split_axis=0, concat_axis=0, tiled=True)
    return pl.pallas_call(
        functools.partial(final_kernel, users, rows_used),
        out_shape=sds((rows, width), BF16),
        in_specs=[vmem] * 3 + [hbm] * 2,
        out_specs=vmem,
        scratch_shapes=[
            pltpu.VMEM((rows, width), BF16),
            pltpu.VMEM((width, width), BF16),
            pltpu.VMEM((users, splits, rows_back, LANES), F32),
            pltpu.SemaphoreType.DMA(()),
            pltpu.SemaphoreType.DMA((CHUNKS,)),
        ],
        cost_estimate=half,
        compiler_params=params,
        name="final",
    )(back.reshape(users, splits, rows_back, LANES), ids, held_back, in_hbm(events),
      in_hbm(out_weight))


def solution(mesh):
    return jax.shard_map(
        functools.partial(on_device, mesh.size, mesh.shape["shard"]),
        mesh=mesh,
        in_specs=(P(AXES, None), P(AXES), P(AXES), P(), P(), P(), P(), P(), P()),
        out_specs=P(AXES, None),
        check_vma=False,
    )
```

```python
import functools

import jax
import jax.numpy as jnp
from jax import lax
from jax.experimental import pallas as pl
from jax.experimental.pallas import tpu as pltpu
from jax.sharding import PartitionSpec as P

U_DEV = 4
LANES = 128
CHUNKS = 4
RADIX = 128.0
VMEM_BYTES = 12 * 2**20
AXES = ("grp", "shard")
F32, BF16 = jnp.float32, jnp.bfloat16


def dot(left, right):
    return jnp.dot(left, right, preferred_element_type=F32)


def dot_t(left, right):
    return lax.dot_general(left, right, (((0,), (0,)), ((), ())), preferred_element_type=F32)


def rms_rows(values):
    return lax.rsqrt(jnp.mean(values * values, axis=-1, keepdims=True) + 1e-06)


def member_rows(ids_row, users):
    user = lax.broadcasted_iota(jnp.int32, (users, ids_row.shape[1]), 0)
    return (user == ids_row).astype(F32)


def row_compare(rows, compare):
    square = (rows, rows)
    return compare(
        lax.broadcasted_iota(jnp.int32, square, 1), lax.broadcasted_iota(jnp.int32, square, 0)
    )


def as_lanes(columns):
    shape = (columns[0].shape[0], LANES)
    lane = lax.broadcasted_iota(jnp.int32, shape, 1)
    total = jnp.zeros(shape, F32)
    for i, column in enumerate(columns):
        total = jnp.where(lane == i, column, total)
    return total


def started(copies):
    for copy in copies:
        copy.start()
    return copies


def weight_copies(hbm, vmem, sem, first):
    chunks = sem.shape[0]
    width = vmem.shape[1] // chunks
    return [
        pltpu.make_async_copy(
            hbm.at[:, pl.ds(first + c * width, width)],
            vmem.at[:, pl.ds(c * width, width)],
            sem.at[c],
        )
        for c in range(chunks)
    ]


def write_message(message, totals, events, breaks):
    width = totals.shape[1]
    message[:, :width] = totals.astype(BF16)
    high_events = jnp.floor(events * (1.0 / RADIX))
    high_breaks = jnp.floor(breaks * (1.0 / RADIX))
    message[:, width:] = as_lanes(
        [high_events, events - RADIX * high_events, high_breaks, breaks - RADIX * high_breaks]
    ).astype(BF16)


def ends_kernel(
    users,
    events_hbm, ids_hbm, breaks_hbm, in_gain_hbm, rates_hbm, keep_hbm, weight_hbm,
    message, totals, counts, normed_out, value_out,
    events, ids, breaks, in_gain, rates, keep, held, small_sem, sem,
):
    rows, width = events.shape
    small = started(
        [
            pltpu.make_async_copy(source, target, small_sem.at[i])
            for i, (source, target) in enumerate(
                (
                    (events_hbm, events),
                    (ids_hbm, ids),
                    (breaks_hbm, breaks),
                    (in_gain_hbm, in_gain),
                    (rates_hbm, rates),
                    (keep_hbm, keep),
                )
            )
        ]
    )
    copies = started(weight_copies(weight_hbm, held, sem, width))
    for copy in small:
        copy.wait()
    break_row = breaks[...].astype(F32)
    member = member_rows(ids[...], users)
    member_b = member.astype(BF16)
    later = jnp.where(row_compare(rows, jnp.greater), dot_t(member_b, member_b), 0.0)
    events_left = jnp.sum(later, axis=1, keepdims=True)
    breaks_left = jnp.sum(later * break_row, axis=1, keepdims=True)
    user_events = jnp.sum(member, axis=1, keepdims=True)
    user_breaks = jnp.sum(member * break_row, axis=1, keepdims=True)
    counts[...] = as_lanes([user_events, user_breaks])
    event_rows = events[...].astype(F32)
    normed = (event_rows * rms_rows(event_rows) * in_gain[...]).astype(BF16)
    normed_out[...] = normed
    block = width // CHUNKS
    for c in range(CHUNKS):
        cols = pl.ds(c * block, block)
        fade = jnp.exp(-rates[:, cols] * events_left + jnp.log(keep[:, cols]) * breaks_left)
        copies[c].wait()
        value = dot(normed, held[:, cols]).astype(BF16)
        value_out[:, cols] = value
        totals[:, cols] = dot(member_b, (fade * value.astype(F32)).astype(BF16))
    write_message(message, totals[...], user_events, user_breaks)


def gate_kernel(normed, out_gain, weight_hbm, gate_out, held, sem):
    width = normed.shape[1]
    copies = started(weight_copies(weight_hbm, held, sem, 0))
    block = width // CHUNKS
    for c in range(CHUNKS):
        copies[c].wait()
        cols = pl.ds(c * block, block)
        gate = dot(normed[...], held[:, cols]).astype(BF16).astype(F32)
        gate_out[:, cols] = out_gain[:, cols] * (gate / (1.0 + jnp.exp(-gate)))


def local_kernel(users, value, ids, breaks, rates, keep, level_out, local_out):
    rows, width = value.shape
    break_row = breaks[...].astype(F32)
    member_b = member_rows(ids[...], users).astype(BF16)
    within = jnp.where(row_compare(rows, jnp.less_equal), dot_t(member_b, member_b), 0.0)
    count = jnp.sum(within, axis=1, keepdims=True)
    count_breaks = jnp.sum(within * break_row, axis=1, keepdims=True)
    level_out[...] = as_lanes([count, count_breaks])
    within_b = within.astype(BF16)
    within_twice = jnp.concatenate([within_b, within_b], axis=1)
    scaled = jnp.exp(rates[...] * count - jnp.log(keep[...]) * count_breaks) * value[...].astype(F32)
    high = scaled.astype(BF16)
    low = (scaled - high.astype(F32)).astype(BF16)
    local_out[...] = dot(within_twice, jnp.concatenate([high, low], axis=0))


def merged(axis, stride, size, messages, totals, counts, carry, rates, keep, need_totals):
    width = totals.shape[1]
    place = lax.rem(lax.div(lax.axis_index(axis), stride), size)
    rate, log_keep = rates[...], jnp.log(keep[...])
    level = lambda events, breaks: log_keep * breaks - rate * events
    column = lambda array, i: array[:, i:i + 1]
    events, breaks, carry_events, carry_breaks = (column(counts, i) for i in range(4))

    def fold(step, state):
        totals, events, breaks, carry, carry_events, carry_breaks = state
        got = messages[step - 1][...].astype(F32)
        got_totals, digits = got[:, :width], got[:, width:]
        got_events = RADIX * column(digits, 0) + column(digits, 1)
        got_breaks = RADIX * column(digits, 2) + column(digits, 3)
        earlier = (place >= step).astype(F32)
        fade = earlier * jnp.exp(level(carry_events, carry_breaks))
        carry = fade * got_totals if carry is None else carry + fade * got_totals
        if need_totals:
            after = 1.0 - earlier
            totals = (
                jnp.exp(level(earlier * events, earlier * breaks)) * got_totals
                + jnp.exp(level(after * got_events, after * got_breaks)) * totals
            )
        return (
            totals, events + got_events, breaks + got_breaks,
            carry, carry_events + earlier * got_events, carry_breaks + earlier * got_breaks,
        )

    state = (totals, events, breaks, carry, carry_events, carry_breaks)
    for step in range(1, size):
        state = fold(step, state)
    return state


def merge_kernel(axis, stride, size, fresh, *refs):
    messages, (totals, counts, *rest) = refs[:size - 1], refs[size - 1:]
    carry = None if fresh else rest.pop(0)[...]
    rates, keep, message, totals_out, counts_out, carry_out = rest
    state = merged(
        axis, stride, size, messages, totals[...], counts[...], carry, rates, keep, True
    )
    new_totals, events, breaks, new_carry, carry_events, carry_breaks = state
    write_message(message, new_totals, events, breaks)
    totals_out[...] = new_totals
    counts_out[...] = as_lanes([events, breaks, carry_events, carry_breaks])
    carry_out[...] = new_carry


def final_kernel(axis, stride, size, users, *refs):
    messages, rest = refs[:size - 1], refs[size - 1:]
    totals, counts, carry, rates, keep, ids, level, local, gate, events, weight, out = rest
    width = events.shape[1]
    state = merged(
        axis, stride, size, messages, totals[...], counts[...], carry[...], rates, keep, False
    )
    carried = state[3]
    high = carried.astype(BF16)
    low = (carried - high.astype(F32)).astype(BF16)
    member_b = member_rows(ids[...], users).astype(BF16)
    entering = dot_t(
        jnp.concatenate([member_b, member_b], axis=0), jnp.concatenate([high, low], axis=0)
    )
    growth = jnp.exp(jnp.log(keep[...]) * level[:, 1:2] - rates[...] * level[:, 0:1])
    hidden = growth * (local[...] + entering)
    mixed_part = (hidden * rms_rows(hidden) * gate[...]).astype(BF16)
    block = width // CHUNKS
    for c in range(CHUNKS):
        cols = pl.ds(c * block, block)
        out[:, cols] = (events[:, cols].astype(F32) + dot(mixed_part, weight[:, cols])).astype(BF16)


def exchange_rounds(mesh):
    rounds = []
    for axis in reversed(AXES):
        stride, left, size = 1, mesh.shape[axis], 2
        while left > 1:
            if left % size:
                size += 1
                continue
            rounds.append((axis, stride, size))
            stride, left = stride * size, left // size
    return rounds


def shift_pairs(length, stride, size, step):
    pairs = []
    for source in range(length):
        place = source // stride % size
        pairs.append((source, source + ((place + step) % size - place) * stride))
    return pairs


def on_device(
    mesh_shape,
    rounds,
    events,
    user_ids,
    session_break,
    in_gain,
    in_weight,
    decay_rates,
    keep_factor,
    out_gain,
    out_weight,
):
    rows, width = events.shape
    users = U_DEV * mesh_shape["shard"]
    ids = user_ids.reshape(1, rows)
    breaks = session_break.reshape(1, rows)
    row = lambda vector: vector.reshape(1, width)
    gain, rates, keep = row(in_gain), row(decay_rates), row(keep_factor)
    hbm = pl.BlockSpec(memory_space=pltpu.HBM)
    vmem = pl.BlockSpec(memory_space=pltpu.VMEM)
    in_hbm = lambda value: pltpu.with_memory_space_constraint(value, pltpu.HBM)
    sds = jax.ShapeDtypeStruct
    params = pltpu.CompilerParams(vmem_limit_bytes=VMEM_BYTES)
    matmul_cost = pl.CostEstimate(
        flops=2 * rows * width * width, bytes_accessed=2 * width * width, transcendentals=0
    )
    message_type = sds((users, width + LANES), BF16)
    state_type = sds((users, width), F32)
    counts_type = sds((users, LANES), F32)

    message, totals, counts, normed, value = pl.pallas_call(
        functools.partial(ends_kernel, users),
        out_shape=(
            message_type, state_type, counts_type, sds((rows, width), BF16), sds((rows, width), BF16)
        ),
        in_specs=[hbm] * 7,
        out_specs=(vmem,) * 5,
        scratch_shapes=[
            pltpu.VMEM((rows, width), BF16),
            pltpu.VMEM((1, rows), jnp.int32),
            pltpu.VMEM((1, rows), jnp.int32),
            pltpu.VMEM((1, width), F32),
            pltpu.VMEM((1, width), F32),
            pltpu.VMEM((1, width), F32),
            pltpu.VMEM((width, width), BF16),
            pltpu.SemaphoreType.DMA((6,)),
            pltpu.SemaphoreType.DMA((CHUNKS,)),
        ],
        cost_estimate=matmul_cost,
        compiler_params=params,
        name="ends",
    )(*map(in_hbm, (events, ids, breaks, gain, rates, keep, in_weight)))

    gate = pl.pallas_call(
        gate_kernel,
        out_shape=sds((rows, width), F32),
        in_specs=[vmem] * 2 + [hbm],
        out_specs=vmem,
        scratch_shapes=[pltpu.VMEM((width, width), BF16), pltpu.SemaphoreType.DMA((CHUNKS,))],
        cost_estimate=matmul_cost,
        compiler_params=params,
        name="gate",
    )(normed, row(out_gain), in_hbm(in_weight))
    level, local = pl.pallas_call(
        functools.partial(local_kernel, users),
        out_shape=(sds((rows, LANES), F32), sds((rows, width), F32)),
        in_specs=[vmem] * 5,
        out_specs=(vmem,) * 2,
        cost_estimate=matmul_cost,
        compiler_params=params,
        name="local",
    )(value, ids, breaks, rates, keep)

    carry = ()
    for index, (axis, stride, size) in enumerate(rounds):
        messages = tuple(
            lax.ppermute(message, axis, shift_pairs(mesh_shape[axis], stride, size, step))
            for step in range(1, size)
        )
        if index == len(rounds) - 1:
            break
        message, totals, counts, *carry = pl.pallas_call(
            functools.partial(merge_kernel, axis, stride, size, index == 0),
            out_shape=(message_type, state_type, counts_type, state_type),
            in_specs=[vmem] * (len(messages) + 4 + len(carry)),
            out_specs=(vmem,) * 4,
            compiler_params=params,
            name="merge",
        )(*messages, totals, counts, *carry, rates, keep)
    return pl.pallas_call(
        functools.partial(final_kernel, axis, stride, size, users),
        out_shape=sds((rows, width), BF16),
        in_specs=[vmem] * (len(messages) + 11),
        out_specs=vmem,
        cost_estimate=matmul_cost,
        compiler_params=params,
        name="final",
    )(
        *messages, totals, counts, *carry, rates, keep, ids, level, local, gate, events, out_weight
    )


def solution(mesh):
    return jax.shard_map(
        functools.partial(on_device, dict(mesh.shape), exchange_rounds(mesh)),
        mesh=mesh,
        in_specs=(P(AXES, None), P(AXES), P(AXES), P(), P(), P(), P(), P(), P()),
        out_specs=P(AXES, None),
        check_vma=False,
    )
```

```python
import functools

import jax
import jax.numpy as jnp
from jax import lax
from jax.experimental import pallas as pl
from jax.experimental.pallas import tpu as pltpu
from jax.sharding import PartitionSpec as P

U_DEV = 4
LANES = 128
CHUNKS = 4
GATE_ROUND = 2
SPLIT = (1, 1)
RADIX = 128.0
LOG2_E = 1.4426950408889634
VMEM_BYTES = 12 * 2**20
AXES = ("grp", "shard")
F32, BF16 = jnp.float32, jnp.bfloat16


def dot(left, right):
    return jnp.dot(left, right, preferred_element_type=F32)


def dot_t(left, right):
    return lax.dot_general(left, right, (((0,), (0,)), ((), ())), preferred_element_type=F32)


def rms_rows(values):
    return lax.rsqrt(jnp.mean(values * values, axis=-1, keepdims=True) + 1e-06)


def member_rows(ids_row, users):
    user = lax.broadcasted_iota(jnp.int32, (users, ids_row.shape[1]), 0)
    return (user == ids_row).astype(F32)


def row_compare(rows, compare):
    square = (rows, rows)
    return compare(
        lax.broadcasted_iota(jnp.int32, square, 1), lax.broadcasted_iota(jnp.int32, square, 0)
    )


def as_lanes(columns):
    shape = (columns[0].shape[0], LANES)
    lane = lax.broadcasted_iota(jnp.int32, shape, 1)
    total = jnp.zeros(shape, F32)
    for i, column in enumerate(columns):
        total = jnp.where(lane == i, column, total)
    return total


def started(copies):
    for copy in copies:
        copy.start()
    return copies


def column_spans(width, split):
    unit, spans, start = width // sum(split), [], 0
    for share in split:
        spans.append(pl.ds(start, share * unit))
        start += share * unit
    return spans


def weight_copies(hbm, vmem, sem, spans, first):
    return [
        pltpu.make_async_copy(
            hbm.at[:, pl.ds(first + span.start, span.size)], vmem.at[:, span], sem.at[c]
        )
        for c, span in enumerate(spans)
    ]


def write_counts(message, events, breaks):
    width = message.shape[1] - LANES
    high_events = jnp.floor(events * (1.0 / RADIX))
    high_breaks = jnp.floor(breaks * (1.0 / RADIX))
    message[:, width:] = as_lanes(
        [high_events, events - RADIX * high_events, high_breaks, breaks - RADIX * high_breaks]
    ).astype(BF16)


def fade(levels, cols, events, breaks):
    return jnp.exp2(levels[0:1, cols] * events + levels[1:2, cols] * breaks)


def ends_kernel(
    users,
    events_hbm, ids_hbm, breaks_hbm, in_gain_hbm, rates_hbm, keep_hbm, weight_hbm,
    message, totals, counts, levels, normed_out, value_out,
    events, ids, breaks, in_gain, rates, keep, held, small_sem, sem,
):
    rows, width = events.shape
    small = started(
        [
            pltpu.make_async_copy(source, target, small_sem.at[i])
            for i, (source, target) in enumerate(
                (
                    (ids_hbm, ids),
                    (breaks_hbm, breaks),
                    (rates_hbm, rates),
                    (keep_hbm, keep),
                    (events_hbm, events),
                    (in_gain_hbm, in_gain),
                )
            )
        ]
    )
    spans = column_spans(width, SPLIT)
    copies = started(weight_copies(weight_hbm, held, sem, spans, width))
    for copy in small[:4]:
        copy.wait()
    break_row = breaks[...].astype(F32)
    member = member_rows(ids[...], users)
    member_b = member.astype(BF16)
    later = jnp.where(row_compare(rows, jnp.greater), dot_t(member_b, member_b), 0.0)
    events_left = jnp.sum(later, axis=1, keepdims=True)
    breaks_left = jnp.sum(later * break_row, axis=1, keepdims=True)
    user_events = jnp.sum(member, axis=1, keepdims=True)
    user_breaks = jnp.sum(member * break_row, axis=1, keepdims=True)
    counts[...] = as_lanes([user_events, user_breaks])
    levels[0:1, :] = rates[...] * -LOG2_E
    levels[1:2, :] = jnp.log(keep[...]) * LOG2_E
    write_counts(message, user_events, user_breaks)
    for copy in small[4:]:
        copy.wait()
    event_rows = events[...].astype(F32)
    normed = (event_rows * rms_rows(event_rows) * in_gain[...]).astype(BF16)
    normed_out[...] = normed
    previous = None
    for c in range(len(spans) + 1):
        latest = None
        if c < len(spans):
            copies[c].wait()
            value = dot(normed, held[:, spans[c]]).astype(BF16)
            value_out[:, spans[c]] = value
            latest = value, fade(levels, spans[c], events_left, breaks_left)
        if c > 0:
            value, faded = previous
            ends = dot(member_b, (faded * value.astype(F32)).astype(BF16))
            totals[:, spans[c - 1]] = ends
            message[:, spans[c - 1]] = ends.astype(BF16)
        previous = latest


def gate_kernel(normed, out_gain, _, weight_hbm, gate_out, done, held, sem):
    width = normed.shape[1]
    spans = column_spans(width, SPLIT)
    copies = started(weight_copies(weight_hbm, held, sem, spans, 0))
    for copy, cols in zip(copies, spans):
        copy.wait()
        gate = dot(normed[...], held[:, cols]).astype(BF16).astype(F32)
        gate_out[:, cols] = out_gain[:, cols] * (gate / (1.0 + jnp.exp(-gate)))
    done[...] = jnp.zeros_like(done)


def local_kernel(users, value, ids, breaks, levels, growth_out, local_out):
    rows, width = value.shape
    break_row = breaks[...].astype(F32)
    member_b = member_rows(ids[...], users).astype(BF16)
    within = jnp.where(row_compare(rows, jnp.less_equal), dot_t(member_b, member_b), 0.0)
    count = jnp.sum(within, axis=1, keepdims=True)
    count_breaks = jnp.sum(within * break_row, axis=1, keepdims=True)
    within_b = within.astype(BF16)
    within_twice = jnp.concatenate([within_b, within_b], axis=1)
    scaled = fade(levels, slice(None), -count, -count_breaks) * value[...].astype(F32)
    high = scaled.astype(BF16)
    low = (scaled - high.astype(F32)).astype(BF16)
    growth = fade(levels, slice(None), count, count_breaks)
    growth_out[...] = growth
    local_out[...] = growth * dot(within_twice, jnp.concatenate([high, low], axis=0))


def received(message):
    got = message[...].astype(F32)
    sums, digits = got[:, :-LANES], got[:, -LANES:]
    column = lambda i: digits[:, i:i + 1]
    return sums, RADIX * column(0) + column(1), RADIX * column(2) + column(3)


def joined(levels, first, second):
    if first is None or second is None:
        return second if first is None else first
    return (
        fade(levels, slice(None), second[1], second[2]) * first[0] + second[0],
        first[1] + second[1],
        first[2] + second[2],
    )


def place_of(axis, stride, size):
    return lax.rem(lax.div(lax.axis_index(axis), stride), size)


def merge_kernel(axis, stride, size, fresh, *refs):
    messages, (totals, counts, *rest) = refs[:size - 1], refs[size - 1:]
    carry_in = None if fresh else rest.pop(0)
    levels, _, message, counts_out, carry_out, *totals_out = rest

    def folded(place):
        column = lambda i: counts[:, i:i + 1]
        own = (totals[...], column(0), column(1))
        carry = None if fresh else (carry_in[...], column(2), column(3))
        blocks = [received(ref) for ref in messages]
        for block in blocks[:place]:
            carry = joined(levels, block, carry)
            own = joined(levels, block, own)
        for block in reversed(blocks[place:]):
            own = joined(levels, own, block)
        if carry is None:
            carry = (jnp.zeros_like(own[0]), jnp.zeros_like(own[1]), jnp.zeros_like(own[2]))
        message[:, :totals.shape[1]] = own[0].astype(BF16)
        write_counts(message, own[1], own[2])
        if totals_out:
            totals_out[0][...] = own[0]
        counts_out[...] = as_lanes([own[1], own[2], carry[1], carry[2]])
        carry_out[...] = carry[0]

    for place in range(size):
        pl.when(place_of(axis, stride, size) == place)(functools.partial(folded, place))


def final_kernel(axis, stride, size, users, *refs):
    messages, rest = refs[:size - 1], refs[size - 1:]
    counts, carry, levels, ids, growth, local, gate, events, weight, out_hbm, out, sem = rest
    width = events.shape[1]
    place = place_of(axis, stride, size)
    block = (carry[...], counts[:, 2:3], counts[:, 3:4])
    for m, message in enumerate(messages, 1):
        block = joined(levels, [jnp.where(place >= m, a, 0.0) for a in received(message)], block)
    high = block[0].astype(BF16)
    low = (block[0] - high.astype(F32)).astype(BF16)
    member_b = member_rows(ids[...], users).astype(BF16)
    entering = dot_t(
        jnp.concatenate([member_b, member_b], axis=0), jnp.concatenate([high, low], axis=0)
    )
    hidden = local[...] + growth[...] * entering
    mixed_part = (hidden * rms_rows(hidden) * gate[...]).astype(BF16)
    copies = []
    for c, cols in enumerate(column_spans(width, (1,) * CHUNKS)):
        out[:, cols] = (events[:, cols].astype(F32) + dot(mixed_part, weight[:, cols])).astype(BF16)
        copies.append(pltpu.make_async_copy(out.at[:, cols], out_hbm.at[:, cols], sem.at[c]))
        copies[c].start()
    for copy in copies:
        copy.wait()


def exchange_rounds(mesh):
    rounds = []
    for axis in reversed(AXES):
        stride, left = 1, mesh.shape[axis]
        for size in range(2, left + 1):
            while left % size == 0:
                rounds.append((axis, stride, size))
                stride, left = stride * size, left // size
    return rounds


def exchange_pairs(length, stride, size, step):
    pairs = []
    for source in range(length):
        place = source // stride % size
        target = (place + step) % size
        pairs.append((source, source + (target - place) * stride))
    return pairs


def on_device(
    mesh_shape,
    rounds,
    events,
    user_ids,
    session_break,
    in_gain,
    in_weight,
    decay_rates,
    keep_factor,
    out_gain,
    out_weight,
):
    rows, width = events.shape
    users = U_DEV * mesh_shape["shard"]
    ids = user_ids.reshape(1, rows)
    breaks = session_break.reshape(1, rows)
    row = lambda vector: vector.reshape(1, width)
    gain, rates, keep = row(in_gain), row(decay_rates), row(keep_factor)
    hbm = pl.BlockSpec(memory_space=pltpu.HBM)
    vmem = pl.BlockSpec(memory_space=pltpu.VMEM)
    in_hbm = lambda value: pltpu.with_memory_space_constraint(value, pltpu.HBM)
    sds = jax.ShapeDtypeStruct
    params = pltpu.CompilerParams(vmem_limit_bytes=VMEM_BYTES)
    matmul_cost = pl.CostEstimate(
        flops=2 * rows * width * width, bytes_accessed=2 * width * width, transcendentals=0
    )
    message_type = sds((users, width + LANES), BF16)
    state_type = sds((users, width), F32)
    counts_type = sds((users, LANES), F32)

    message, totals, counts, levels, normed, value = pl.pallas_call(
        functools.partial(ends_kernel, users),
        out_shape=(
            message_type, state_type, counts_type, sds((2, width), F32),
            sds((rows, width), BF16), sds((rows, width), BF16),
        ),
        in_specs=[hbm] * 7,
        out_specs=(vmem,) * 6,
        scratch_shapes=[
            pltpu.VMEM((rows, width), BF16),
            pltpu.VMEM((1, rows), jnp.int32),
            pltpu.VMEM((1, rows), jnp.int32),
            pltpu.VMEM((1, width), F32),
            pltpu.VMEM((1, width), F32),
            pltpu.VMEM((1, width), F32),
            pltpu.VMEM((width, width), BF16),
            pltpu.SemaphoreType.DMA((6,)),
            pltpu.SemaphoreType.DMA((len(SPLIT),)),
        ],
        cost_estimate=matmul_cost,
        compiler_params=params,
        name="ends",
    )(*map(in_hbm, (events, ids, breaks, gain, rates, keep, in_weight)))
    growth, local = pl.pallas_call(
        functools.partial(local_kernel, users),
        out_shape=(sds((rows, width), F32),) * 2,
        in_specs=[vmem] * 4,
        out_specs=(vmem,) * 2,
        cost_estimate=matmul_cost,
        compiler_params=params,
        name="local",
    )(value, ids, breaks, levels)

    carry = ()
    done = counts
    last = len(rounds) - 1
    for index, (axis, stride, size) in enumerate(rounds):
        messages = tuple(
            lax.ppermute(message, axis, exchange_pairs(mesh_shape[axis], stride, size, step))
            for step in range(1, size)
        )
        if index == GATE_ROUND:
            gate, done = pl.pallas_call(
                gate_kernel,
                out_shape=(sds((rows, width), F32), sds((8, LANES), F32)),
                in_specs=[vmem] * 3 + [hbm],
                out_specs=(vmem, vmem),
                scratch_shapes=[
                    pltpu.VMEM((width, width), BF16), pltpu.SemaphoreType.DMA((len(SPLIT),))
                ],
                cost_estimate=matmul_cost,
                compiler_params=params,
                name="gate",
            )(normed, row(out_gain), counts, in_hbm(in_weight))
        if index == last:
            break
        out_types = (message_type, counts_type, state_type) + (state_type,) * (index + 1 < last)
        message, counts, *state = pl.pallas_call(
            functools.partial(merge_kernel, axis, stride, size, index == 0),
            out_shape=out_types,
            in_specs=[vmem] * (len(messages) + 4 + len(carry)),
            out_specs=(vmem,) * len(out_types),
            compiler_params=params,
            name="merge",
        )(*messages, totals, counts, *carry, levels, done)
        carry, totals, done = state[:1], state[-1], counts
    return pl.pallas_call(
        functools.partial(final_kernel, axis, stride, size, users),
        out_shape=sds((rows, width), BF16),
        in_specs=[vmem] * (len(messages) + 9),
        out_specs=hbm,
        scratch_shapes=[pltpu.VMEM((rows, width), BF16), pltpu.SemaphoreType.DMA((CHUNKS,))],
        cost_estimate=matmul_cost,
        compiler_params=params,
        name="final",
    )(*messages, counts, *carry, levels, ids, growth, local, gate, events, out_weight)


def solution(mesh):
    return jax.shard_map(
        functools.partial(on_device, dict(mesh.shape), exchange_rounds(mesh)),
        mesh=mesh,
        in_specs=(P(AXES, None), P(AXES), P(AXES), P(), P(), P(), P(), P(), P()),
        out_specs=P(AXES, None),
        check_vma=False,
    )
```
